256 devices in a mesh: sec: 2 (over z_lo), lat: 8 (over y, core), lon: 16 (over z_hi, x).
Axes of the slice: x: 4, y: 4, z: 8 (z_hi: 4, z_lo: 2; z = z_hi * 2 + z_lo), core: 2. Of those that a mesh axis runs over, the one named last changes fastest.
Arguments:
- ocean_state: bfloat16 [4, 2, 8, 32, 128], P(None, 'sec', 'lat', 'lon'), may hold values from -4 to 4
- sea_tiles: int32 [2, 8, 32], P('sec', 'lat', 'lon'), may hold values 0 or 1
- regrid_weights: bfloat16 [64, 4, 128, 4096], P('lat', None, None, 'lon'), may hold values from -0.25 to 0.25
- regrid_src: int32 [64, 16, 4], P('lat', 'lon'), may hold values from 0 to 11
- row_points: int32 [64], P('lat'), may hold values from 1040 to 4096, as said below
- wind: float32 [2, 64, 4096], P(None, 'lat', 'lon'), may hold values from -3 to 3
- conc: bfloat16 [32, 20, 64, 4096], P(None, 'sec', 'lat', 'lon'), may hold values from 0.049804688 to 2
- kdiff: float32 [32, 64, 4096], P(None, 'lat', 'lon'), may hold values from 0.1 to 10
- bin_emit: float32 [20], P('sec'), may hold values from 0.05 to 0.5
- bin_settle: float32 [20], P('sec'), may hold values from 0.1 to 2
- bin_mass: float32 [20], P('sec'), may hold values from 0.2 to 2
Outputs:
- spectra: float32 [32, 20, 64, 2, 1280], P('lon', 'sec', 'lat')
- salt_flux: float32 [64, 4096], P('lat', 'lon')
The draws below stay inside these ranges and needn't reach their ends.
Inputs may be any that keep to these rules, and one draw needn't show every extreme that they name: `regrid_src`: slot k names ocean section k // 6, tile offset (k // 2) % 3 - 1 and block k % 2. `row_points`: a multiple of 16.
All inputs are finite; a program needn't handle non-finite values. No bound on the sum of `sea_tiles` on one device may be relied on, other than what follows from the above.
Results may differ from the reference program's by a relative error of at most 0.0019.
Values may be sent and summed in bfloat16 or wider, within the bound.
A program may use at most 128 MiB of HBM per device.

```python
import math
import jax
import jax.numpy as jnp
from jax import lax

NB = 20
M = 4096
K = 1280
LEV = 32
SB = 128
S = 4
ROWS = 8
NROWS = 64
OB_DEV = 2
OSEC = 2
BANDS = 8
LONS = 16
OLON = 32
N_SEC = 2
N_LAT = 8
N_LON = 16


def draw_row_points(key, part):
    key_steps, key_full = jax.random.split(key, 2)
    steps_down = jax.random.randint(key_steps, (NROWS,), 0, 3 * M // 64)
    lengths = M - 16 * steps_down
    full_row = jax.random.randint(key_full, (), 0, NROWS)
    row_ids = jnp.arange(NROWS)
    lengths = jnp.where(row_ids == full_row, M, lengths)
    lengths = jnp.where(row_ids == (full_row + 1) % NROWS, M // 4 + 16, lengths)
    return lengths.astype(jnp.int32)


def plant(array, key, low, largest):
    longest = array.shape.index(max(array.shape))
    spots = []
    for shift in (0, 1):
        where = [jax.random.randint(jax.random.fold_in(key, axis), (), 0, length) for axis, length in enumerate(array.shape)]
        where[longest] = (where[longest] + shift) % array.shape[longest]
        spots.append(tuple(where))
    return array.at[spots[0]].set(low).at[spots[1]].set(largest)


def levels(own_key, shape, shards, least, high):
    level = 1.0
    for dim, blocks in shards:
        steps = jax.random.uniform(jax.random.fold_in(jax.random.fold_in(own_key, 6), dim), (blocks,), jnp.float32, least / len(shards), high / len(shards))
        level = level * jnp.repeat(jnp.exp(steps), shape[dim] // blocks).reshape((-1,) + (1,) * (len(shape) - 1 - dim))
    return level


def centred(key, shape, scale, bound, shards=(), held_as=jnp.bfloat16):
    entries = jax.random.normal(key, shape, jnp.float32) * scale
    if len(shards) > 0:
        entries = levels(key, shape, shards, -0.22, 0.18) * entries
    return jnp.clip(entries, min=-bound, max=bound).astype(held_as)


def setup_inputs(seed: int = 0) -> dict:
    splits = jax.random.split(jax.random.key(seed), 12)
    return {
        "ocean_state": centred(splits[0], (4, OSEC, BANDS, OLON, SB), 1.0, 4.0, ((1, 2), (2, 8), (3, 16))),
        "sea_tiles": plant((jax.random.randint(splits[1], (OSEC, BANDS, OLON), 0, 4) < 3).astype(jnp.int32), jax.random.fold_in(splits[1], 1), 0, 1),
        "regrid_weights": centred(splits[2], (NROWS, S, SB, M), (S * SB) ** -0.5, 0.25, ((0, 8), (3, 16))),
        "regrid_src": plant(jax.random.randint(splits[3], (NROWS, LONS, S), 0, 6 * OB_DEV), jax.random.fold_in(splits[3], 1), 0, (6 * OB_DEV) - 1).astype(jnp.int32),
        "row_points": draw_row_points(jax.random.fold_in(splits[11], 71), 0),
        "wind": centred(splits[5], (2, NROWS, M), 0.7, 3.0, ((1, 8), (2, 16)), jnp.float32),
        "conc": jnp.clip(jnp.exp(math.log(2.0) - 3.6927934 * jax.random.uniform(splits[6], (LEV, NB, NROWS, M), jnp.float32) ** levels(splits[6], (LEV, NB, NROWS, M), ((1, 2), (2, 8), (3, 16)), -0.2, 0.2)), 0.049804688, 2.0).astype(jnp.bfloat16),
        "kdiff": jnp.clip(jnp.exp(math.log(10.0) - 4.6051702 * jax.random.uniform(splits[7], (LEV, NROWS, M), jnp.float32) ** levels(splits[7], (LEV, NROWS, M), ((1, 8), (2, 16)), -0.2, 0.2)), 0.1, 10.0),
        "bin_emit": jnp.clip(jnp.exp(math.log(0.5) - 2.3025851 * jax.random.uniform(splits[8], (NB,), jnp.float32) ** levels(splits[8], (NB,), ((0, 2),), -0.2, 0.2)), 0.05, 0.5),
        "bin_settle": jnp.clip(jnp.exp(math.log(2.0) - 2.9957323 * jax.random.uniform(splits[9], (NB,), jnp.float32) ** levels(splits[9], (NB,), ((0, 2),), -0.2, 0.2)), 0.1, 2.0),
        "bin_mass": jnp.clip(jnp.exp(math.log(2.0) - 2.3025851 * jax.random.uniform(splits[10], (NB,), jnp.float32) ** levels(splits[10], (NB,), ((0, 2),), -0.2, 0.2)), 0.2, 2.0),
    }


def solve_columns(concentration, kdiff, bin_flux, settle_rate):
    levels_count = concentration.shape[0]
    below_kdiff = jnp.concatenate([kdiff[1:], jnp.zeros_like(kdiff[:1])], axis=0)
    layer_ids = jnp.arange(levels_count, dtype=jnp.int32)
    zeros_start = jnp.zeros_like(concentration[0] + bin_flux)

    def forward(carried, inputs):
        ratio_prev, scaled_prev = carried
        level_conc, here_kdiff, next_kdiff, layer_index = inputs
        bottom = layer_index == levels_count - 1
        coupling = jnp.where(bottom, 0.0, next_kdiff)
        diagonal = 1.0 + here_kdiff + jnp.where(bottom, settle_rate, next_kdiff)
        right_side = level_conc + jnp.where(bottom, bin_flux, 0.0)
        pivots = diagonal - here_kdiff * ratio_prev
        ratio_now = coupling / pivots
        scaled_now = (right_side + here_kdiff * scaled_prev) / pivots
        return ((ratio_now, scaled_now), (ratio_now, scaled_now))
    unused, (ratios, scaled) = lax.scan(forward, (zeros_start, zeros_start), (concentration, kdiff, below_kdiff, layer_ids))

    def backward(carried, inputs):
        ratio_now, scaled_now = inputs
        value_now = scaled_now + ratio_now * carried
        return (value_now, value_now)
    unused, mixed = lax.scan(backward, zeros_start, (ratios, scaled), reverse=True)
    return mixed

def emission_base(fields, wind, valid):
    rel_east = wind[0] - 0.5 * fields[2]
    rel_north = wind[1] - 0.5 * fields[3]
    wind_speed = jnp.sqrt(rel_east * rel_east + rel_north * rel_north + 0.25)
    open_water = 1.0 - jax.nn.sigmoid(fields[1])
    return open_water * jnp.exp(3.41 * jnp.log(wind_speed)) * (0.5 + jax.nn.sigmoid(fields[0])) * valid

def reference(ocean_state, sea_tiles, regrid_weights, regrid_src, row_points, wind, conc, kdiff, bin_emit, bin_settle, bin_mass):
    points_dev = M // N_LON
    blocks_dev = ocean_state.shape[3] // N_LON
    masked = ocean_state.astype(jnp.float32) * sea_tiles[None, :, :, :, None].astype(jnp.float32)
    ocean_grid = masked.reshape(4, N_SEC, N_LAT, N_LON, blocks_dev, SB)
    nearby = jnp.stack([jnp.roll(ocean_grid, 1, axis=3), ocean_grid, jnp.roll(ocean_grid, -1, axis=3)], axis=2)
    nearby = jnp.transpose(nearby, (3, 4, 0, 1, 2, 5, 6)).reshape(N_LAT, N_LON, 4, 6 * blocks_dev, SB)
    row_bands = jnp.arange(NROWS, dtype=jnp.int32) // ROWS
    nearby_rows = nearby[row_bands]
    slot_index = jnp.broadcast_to(regrid_src[:, :, None, :, None], (NROWS, N_LON, 4, S, SB)).astype(jnp.int32)
    chosen = jnp.take_along_axis(nearby_rows, slot_index, axis=3)
    weights = regrid_weights.astype(jnp.float32).reshape(NROWS, S, SB, N_LON, points_dev)
    fields = jnp.einsum('rlfsq,rsqlp->frlp', chosen, weights, precision=lax.Precision.HIGHEST).reshape(4, NROWS, M)
    columns = jnp.arange(M, dtype=jnp.int32)
    valid = (columns[None, :] < row_points[:, None]).astype(jnp.float32)
    base_rate = emission_base(fields, wind, valid)
    conc_bins = jnp.transpose(conc, (1, 0, 2, 3))

    def one_bin(inputs):
        bin_conc, emit_rate, settle_rate, mass_rate = inputs
        bin_flux = emit_rate * base_rate
        mixed = solve_columns(bin_conc.astype(jnp.float32), kdiff, bin_flux, settle_rate)
        net_flux = bin_flux - settle_rate * mixed[LEV - 1]
        salt_term = mass_rate * net_flux
        rounded = lax.optimization_barrier(mixed.astype(jnp.bfloat16))
        spectral_in = rounded.astype(jnp.float32) * valid
        coeffs = jnp.fft.rfft(spectral_in, axis=-1)[..., :K]
        spectrum = jnp.stack([jnp.real(coeffs), jnp.imag(coeffs)], axis=-2) * (1.0 / math.sqrt(M))
        return (spectrum, salt_term)
    spectra_bins, salt_terms = lax.map(one_bin, (conc_bins, bin_emit, bin_settle, bin_mass))
    salt_flux = lax.optimization_barrier(jnp.sum(salt_terms, axis=0)) * valid
    spectra = jnp.transpose(spectra_bins, (1, 0, 2, 3, 4))
    return (spectra, salt_flux)
```

```python
import functools
import math

import jax
import jax.numpy as jnp
import numpy as np
from jax import lax
from jax.experimental import pallas as pl
from jax.experimental.pallas import tpu as pltpu
from jax.sharding import PartitionSpec as P

M = 4096
K = 1280
LEV = 32
TILES = 16
PTS = 256
NBD = 10
ROWS = 8
CHUNK = 2
NCHUNK = NBD // CHUNK
MESH = pl.DeviceIdType.MESH


def mix_kernel(
    ocean_ref,
    sea_ref,
    src_ref,
    points_ref,
    emit_ref,
    settle_ref,
    mass_ref,
    wind_hbm,
    weights_hbm,
    conc_hbm,
    kdiff_hbm,
    recv_hbm,
    salt_ref,
    wind_ref,
    weights_ref,
    conc_ref,
    kdiff_ref,
    near_ref,
    lhs_ref,
    fields_ref,
    ratio_ref,
    scaled_ref,
    out_ref,
    part_ref,
    other_ref,
    local_sem,
    own_sem,
    near_send,
    near_recv,
    salt_send,
    salt_recv,
    a2a_send,
    a2a_recv,
):
    sec = lax.axis_index("sec")
    lat = lax.axis_index("lat")
    lon = lax.axis_index("lon")

    barrier = pltpu.get_barrier_semaphore()
    for step in range(1, TILES):
        peer = lax.rem(lon + step, TILES)
        pl.semaphore_signal(barrier, inc=1, device_id=(sec, lat, peer), device_id_type=MESH)
    for shift in (-1, 0, 1):
        peer = lax.rem(lon + shift + TILES, TILES)
        pl.semaphore_signal(barrier, inc=1, device_id=(1 - sec, lat, peer), device_id_type=MESH)

    loads = [
        pltpu.make_async_copy(kdiff_hbm, kdiff_ref, local_sem.at[0]),
        pltpu.make_async_copy(conc_hbm, conc_ref, local_sem.at[1]),
        pltpu.make_async_copy(weights_hbm, weights_ref, local_sem.at[2]),
        pltpu.make_async_copy(wind_hbm, wind_ref, local_sem.at[3]),
    ]
    for load in loads:
        load.start()

    own_slot = sec * 6 + 2
    ocean = ocean_ref[...].astype(jnp.float32)
    for block in range(2):
        near_ref[own_slot + block] = jnp.zeros((8, 128), jnp.float32)
        sea = sea_ref[0, block].astype(jnp.float32)
        near_ref[own_slot + block, 0:4, :] = ocean[:, block, :] * sea

    pl.semaphore_wait(barrier, TILES - 1 + 3)

    near_copies = []
    index = 0
    for same_sec in (True, False):
        for shift in (-1, 0, 1):
            if same_sec and shift == 0:
                continue
            peer = lax.rem(lon + shift + TILES, TILES)
            to_sec = sec if same_sec else 1 - sec
            copy = pltpu.make_async_remote_copy(
                src_ref=near_ref.at[pl.ds(own_slot, 2)],
                dst_ref=near_ref.at[pl.ds(sec * 6 + (1 - shift) * 2, 2)],
                send_sem=near_send.at[index],
                recv_sem=near_recv.at[index],
                device_id=(to_sec, lat, peer),
                device_id_type=MESH,
            )
            copy.start()
            near_copies.append(copy)
            index += 1

    loads[0].wait()
    loads[1].wait()

    def eliminate(level, carried):
        ratio_prev, scaled_prev = carried
        here = kdiff_ref[level]
        below = kdiff_ref[level + 1]
        inverse = 1.0 / (1.0 + here + below - here * ratio_prev)
        ratio_now = below * inverse
        ratio_ref[level] = ratio_now
        scaled_now = []
        for b in range(NBD):
            value = (conc_ref[level, b].astype(jnp.float32) + here * scaled_prev[b]) * inverse
            scaled_ref[level, b] = value
            scaled_now.append(value)
        return ratio_now, tuple(scaled_now)

    zero = jnp.zeros((ROWS, PTS), jnp.float32)
    ratio_last, scaled_last = lax.fori_loop(0, LEV - 1, eliminate, (zero, (zero,) * NBD))

    row_ids = lax.broadcasted_iota(jnp.int32, (ROWS, PTS), 0)
    columns = lax.broadcasted_iota(jnp.int32, (ROWS, PTS), 1) + lon * PTS
    limits = jnp.zeros((ROWS, PTS), jnp.int32)
    for r in range(ROWS):
        limits = jnp.where(row_ids == r, points_ref[r], limits)
    valid = (columns < limits).astype(jnp.float32)

    loads[2].wait()
    loads[3].wait()
    for copy in near_copies:
        copy.wait()

    for r in range(ROWS):
        for s in range(4):
            lhs_ref[r, :, s * 128 : (s + 1) * 128] = near_ref[src_ref[0, s, r]]
    for r in range(ROWS):
        fields_ref[r] = jnp.dot(
            lhs_ref[r].astype(jnp.bfloat16),
            weights_ref[r].reshape(512, PTS),
            preferred_element_type=jnp.float32,
        )
    temp = fields_ref[:, 0, :]
    ice = fields_ref[:, 1, :]
    rel_east = wind_ref[0] - 0.5 * fields_ref[:, 2, :]
    rel_north = wind_ref[1] - 0.5 * fields_ref[:, 3, :]
    speed = jnp.sqrt(rel_east * rel_east + rel_north * rel_north + 0.25)
    base = (
        (1.0 - jax.nn.sigmoid(ice))
        * jnp.exp(3.41 * jnp.log(speed))
        * (0.5 + jax.nn.sigmoid(temp))
        * valid
    )

    last_kdiff = kdiff_ref[LEV - 1]
    pivot_part = 1.0 + last_kdiff - last_kdiff * ratio_last
    partial = zero
    for b in range(NBD):
        flux = emit_ref[b] * base
        settle = settle_ref[b]
        value = (
            conc_ref[LEV - 1, b].astype(jnp.float32) + flux + last_kdiff * scaled_last[b]
        ) / (pivot_part + settle)
        scaled_ref[LEV - 1, b] = value
        partial = partial + mass_ref[b] * (flux - settle * value)
    part_ref[...] = partial

    salt_copy = pltpu.make_async_remote_copy(
        src_ref=part_ref,
        dst_ref=other_ref,
        send_sem=salt_send,
        recv_sem=salt_recv,
        device_id=(1 - sec, lat, lon),
        device_id_type=MESH,
    )

    def a2a_copy(chunk, step):
        peer = lax.rem(lon + step, TILES)
        bins = pl.ds(chunk * CHUNK, CHUNK)
        return pltpu.make_async_remote_copy(
            src_ref=out_ref.at[pl.ds(peer * 2, 2), bins],
            dst_ref=recv_hbm.at[lon, :, bins],
            send_sem=a2a_send.at[chunk, step],
            recv_sem=a2a_recv.at[chunk, step],
            device_id=(sec, lat, peer),
            device_id_type=MESH,
        )

    def own_copy(chunk):
        bins = pl.ds(chunk * CHUNK, CHUNK)
        return pltpu.make_async_copy(
            out_ref.at[pl.ds(lon * 2, 2), bins], recv_hbm.at[lon, :, bins], own_sem.at[chunk]
        )

    keep = valid > 0.0
    for chunk in range(NCHUNK):
        first = chunk * CHUNK
        start = tuple(scaled_ref[LEV - 1, first + b] for b in range(CHUNK))
        for b in range(CHUNK):
            out_ref[LEV - 1, first + b] = jnp.where(keep, start[b], 0.0).astype(jnp.bfloat16)

        def substitute(count, carried, first=first):
            level = LEV - 2 - count
            ratio = ratio_ref[level]
            values = []
            for b in range(CHUNK):
                value = scaled_ref[level, first + b] + ratio * carried[b]
                out_ref[level, first + b] = jnp.where(keep, value, 0.0).astype(jnp.bfloat16)
                values.append(value)
            return tuple(values)

        lax.fori_loop(0, LEV - 1, substitute, start)
        if chunk == 0:
            salt_copy.start()

        @pl.loop(1, TILES)
        def _(step, chunk=chunk):
            a2a_copy(chunk, step).start()

        own_copy(chunk).start()

    salt_copy.wait()
    salt_ref[...] = (part_ref[...] + other_ref[...]) * valid

    for chunk in range(NCHUNK):
        own_copy(chunk).wait()

        @pl.loop(1, TILES)
        def _(step, chunk=chunk):
            a2a_copy(chunk, step).wait()


def mix_and_exchange(ocean, sea, src, points, emit, settle, mass, wind, weights, conc, kdiff):
    vmem = pl.BlockSpec(memory_space=pltpu.VMEM)
    smem = pl.BlockSpec(memory_space=pltpu.SMEM)
    anywhere = pl.BlockSpec(memory_space=pl.ANY)
    dma = pltpu.SemaphoreType.DMA
    return pl.pallas_call(
        mix_kernel,
        name="mix_and_exchange",
        out_shape=(
            jax.ShapeDtypeStruct((TILES, 2, NBD, ROWS, PTS), jnp.bfloat16),
            jax.ShapeDtypeStruct((ROWS, PTS), jnp.float32),
        ),
        in_specs=[vmem] + [smem] * 6 + [anywhere] * 4,
        out_specs=(anywhere, vmem),
        scratch_shapes=[
            pltpu.VMEM((2, ROWS, PTS), jnp.float32),
            pltpu.VMEM((ROWS, 4, 128, PTS), jnp.bfloat16),
            pltpu.VMEM((LEV, NBD, ROWS, PTS), jnp.bfloat16),
            pltpu.VMEM((LEV, ROWS, PTS), jnp.float32),
            pltpu.VMEM((12, 8, 128), jnp.float32),
            pltpu.VMEM((ROWS, 8, 512), jnp.float32),
            pltpu.VMEM((ROWS, 8, PTS), jnp.float32),
            pltpu.VMEM((LEV, ROWS, PTS), jnp.float32),
            pltpu.VMEM((LEV, NBD, ROWS, PTS), jnp.float32),
            pltpu.VMEM((LEV, NBD, ROWS, PTS), jnp.bfloat16),
            pltpu.VMEM((ROWS, PTS), jnp.float32),
            pltpu.VMEM((ROWS, PTS), jnp.float32),
            dma((4,)),
            dma((NCHUNK,)),
            dma((5,)),
            dma((5,)),
            dma,
            dma,
            dma((NCHUNK, TILES)),
            dma((NCHUNK, TILES)),
        ],
        compiler_params=pltpu.CompilerParams(collective_id=0, has_side_effects=True),
    )(ocean, sea, src, points, emit, settle, mass, wind, weights, conc, kdiff)


def twiddles():
    phase = np.arange(TILES)[:, None] * np.arange(PTS)[None, :] * (2.0 * np.pi / M)
    parts = np.stack([np.cos(phase), np.sin(phase)], axis=1) * (1.0 / math.sqrt(M))
    return parts.astype(np.float32)


def row_table():
    column = np.arange(256)
    combo = (column // 128) * 16 + column % 16
    ka = 8 * (combo // 2) + (column % 128) // 16
    phase = np.arange(PTS)[:, None] * ka[None, :] % PTS * (2.0 * np.pi / PTS)
    cos, sin = np.cos(phase), np.sin(phase)
    is_cos = (combo % 2 == 0)[None, :]
    upper = np.where(is_cos, cos, -sin)
    lower = np.where(is_cos, -sin, -cos)
    table = np.concatenate([upper, lower], axis=0) * (combo < 20)[None, :]
    return table.astype(np.float32)


def real_dft16(x):
    c1, c2, c3 = math.cos(math.pi / 8), math.cos(math.pi / 4), math.cos(3 * math.pi / 8)
    s = [x[i] + x[i + 8] for i in range(8)]
    d = [x[i] - x[i + 8] for i in range(8)]
    a = [s[i] + s[i + 4] for i in range(4)]
    b = [s[i] - s[i + 4] for i in range(4)]
    out = [None] * 9
    a02, a13 = a[0] + a[2], a[1] + a[3]
    out[0] = (a02 + a13, None)
    out[8] = (a02 - a13, None)
    out[4] = (a[0] - a[2], a[1] - a[3])
    bm, bp = (b[1] - b[3]) * c2, (b[1] + b[3]) * c2
    out[2] = (b[0] + bm, bp + b[2])
    out[6] = (b[0] - bm, bp - b[2])
    e1, e2, e3 = d[1] - d[7], (d[2] - d[6]) * c2, d[3] - d[5]
    f1, f2, f3 = d[1] + d[7], (d[2] + d[6]) * c2, d[3] + d[5]
    p, q = d[0] + e2, d[0] - e2
    u, v = e1 * c1 + e3 * c3, e1 * c3 - e3 * c1
    g, h = f1 * c3 + f3 * c1, f1 * c1 - f3 * c3
    m, n = f2 + d[4], f2 - d[4]
    out[1] = (p + u, g + m)
    out[7] = (p - u, g - m)
    out[3] = (q + v, h + n)
    out[5] = (q - v, h - n)
    return out


def transform_kernel(x_ref, twiddle_ref, table_ref, salt_in_ref, y_ref, salt_ref, z_ref, o_ref):
    salt_ref[...] = salt_in_ref[...]
    for half in range(2):
        lanes = slice(half * 128, (half + 1) * 128)
        x = [
            x_ref[tile, 0, :, :, lanes].astype(jnp.float32).reshape(16, 128)
            for tile in range(TILES)
        ]
        coefficients = real_dft16(x)
        for kb in range(TILES):
            re, im = coefficients[min(kb, TILES - kb)]
            cos = twiddle_ref[kb, 0:1, lanes]
            sin = twiddle_ref[kb, 1:2, lanes]
            if im is None:
                real, minus = re * cos, re * sin
            elif kb < 8:
                real, minus = re * cos - im * sin, re * sin + im * cos
            else:
                real, minus = re * cos + im * sin, re * sin - im * cos
            z_ref[kb, :, half * 128 : (half + 1) * 128] = real.astype(jnp.bfloat16)
            z_ref[kb, :, PTS + half * 128 : PTS + (half + 1) * 128] = minus.astype(jnp.bfloat16)
    o_ref[...] = jnp.dot(
        z_ref[...].reshape(TILES * 16, 2 * PTS), table_ref[...], preferred_element_type=jnp.float32
    ).reshape(TILES, 16, 256)
    lane = lax.broadcasted_iota(jnp.int32, (8, 128), 1)
    for group in range(2):
        for q in range(2):
            combos = 16 if q == 0 else 4
            arrays = {
                kb: pltpu.roll(
                    o_ref[kb, group * 8 : (group + 1) * 8, q * 128 : (q + 1) * 128], kb, axis=1
                )
                for kb in range(TILES)
            }
            wanted = {(-t) % TILES for t in range(combos)}
            needs = [wanted]
            for bit in (0, 1, 2):
                wanted = wanted | {(j + (1 << bit)) % TILES for j in wanted}
                needs.append(wanted)
            for bit in (3, 2, 1, 0):
                taken = (lane & (1 << bit)) != 0
                arrays = {
                    j: jnp.where(taken, arrays[(j + (1 << bit)) % TILES], arrays[j])
                    for j in needs[bit]
                }
            for t in range(combos):
                value = arrays[(-t) % TILES]
                if t:
                    value = pltpu.roll(value, 128 - t, axis=1)
                c, part = divmod(q * 16 + t, 2)
                y_ref[0, group, :, part, c * 128 : (c + 1) * 128] = value


def transform(received, salt):
    whole = lambda *shape: pl.BlockSpec(shape, lambda i, j: (0,) * len(shape))
    return pl.pallas_call(
        transform_kernel,
        name="transform",
        grid=(2, NBD // 2),
        out_shape=(
            jax.ShapeDtypeStruct((2, NBD, ROWS, 2, K), jnp.float32),
            jax.ShapeDtypeStruct((ROWS, PTS), jnp.float32),
        ),
        in_specs=[
            pl.BlockSpec((TILES, 1, 2, ROWS, PTS), lambda i, j: (0, i, j, 0, 0)),
            whole(TILES, 2, PTS),
            whole(2 * PTS, 256),
            whole(ROWS, PTS),
        ],
        out_specs=(
            pl.BlockSpec((1, 2, ROWS, 2, K), lambda i, j: (i, j, 0, 0, 0)),
            whole(ROWS, PTS),
        ),
        scratch_shapes=[
            pltpu.VMEM((TILES, 16, 2 * PTS), jnp.bfloat16),
            pltpu.VMEM((TILES, 16, 256), jnp.float32),
        ],
    )(received, jnp.asarray(twiddles()), jnp.asarray(row_table()).astype(jnp.bfloat16), salt)


def on_device(
    ocean_state,
    sea_tiles,
    regrid_weights,
    regrid_src,
    row_points,
    wind,
    conc,
    kdiff,
    bin_emit,
    bin_settle,
    bin_mass,
):
    received, salt = mix_and_exchange(
        ocean_state.reshape(4, 2, 128),
        sea_tiles.reshape(1, 2),
        jnp.transpose(regrid_src, (1, 2, 0)),
        row_points,
        bin_emit,
        bin_settle,
        bin_mass,
        wind,
        regrid_weights,
        conc,
        kdiff,
    )
    return transform(received, salt)


def solution(mesh):
    return jax.shard_map(
        on_device,
        mesh=mesh,
        in_specs=(
            P(None, "sec", "lat", "lon", None),
            P("sec", "lat", "lon"),
            P("lat", None, None, "lon"),
            P("lat", "lon", None),
            P("lat"),
            P(None, "lat", "lon"),
            P(None, "sec", "lat", "lon"),
            P(None, "lat", "lon"),
            P("sec"),
            P("sec"),
            P("sec"),
        ),
        out_specs=(P("lon", "sec", "lat", None, None), P("lat", "lon")),
        check_vma=False,
    )
```

```python
import functools
import math

import jax
import jax.numpy as jnp
import numpy as np
from jax import lax
from jax.experimental import pallas as pl
from jax.experimental.pallas import tpu as pltpu
from jax.sharding import PartitionSpec as P

M = 4096
K = 1280
LEV = 32
TILES = 16
PTS = 256
NBD = 10
ROWS = 8
CHUNK = 2
NCHUNK = NBD // CHUNK
ORDER = (8, 4, 12, 6, 10, 7, 9, 5, 11, 3, 13, 2, 14, 1, 15)
MESH = pl.DeviceIdType.MESH


def fused_kernel(
    ocean_hbm,
    sea_hbm,
    src_hbm,
    points_hbm,
    emit_hbm,
    settle_hbm,
    mass_hbm,
    wind_hbm,
    weights_hbm,
    conc_hbm,
    kdiff_hbm,
    twiddle_hbm,
    table_hbm,
    spectra_hbm,
    salt_ref,
    ocean_ref,
    sea_ref,
    src_ref,
    points_ref,
    emit_ref,
    settle_ref,
    mass_ref,
    wind_ref,
    weights_ref,
    conc_ref,
    kdiff_ref,
    twiddle_ref,
    table_ref,
    near_ref,
    lhs_ref,
    fields_ref,
    ratio_ref,
    scaled_ref,
    out_ref,
    recv_ref,
    part_ref,
    other_ref,
    z_ref,
    o_ref,
    y_ref,
    local_sem,
    own_sem,
    near_send,
    near_recv,
    salt_send,
    salt_recv,
    a2a_send,
    a2a_recv,
    y_sem,
):
    sec = lax.axis_index("sec")
    lat = lax.axis_index("lat")
    lon = lax.axis_index("lon")

    barrier = pltpu.get_barrier_semaphore()
    for step in range(1, TILES):
        peer = lax.rem(lon + step, TILES)
        pl.semaphore_signal(barrier, inc=1, device_id=(sec, lat, peer), device_id_type=MESH)
    for shift in (-1, 0, 1):
        peer = lax.rem(lon + shift + TILES, TILES)
        pl.semaphore_signal(barrier, inc=1, device_id=(1 - sec, lat, peer), device_id_type=MESH)

    ocean_load, sea_load, src_load, points_load, *rest = [
        pltpu.make_async_copy(source, target, local_sem.at[i])
        for i, (source, target) in enumerate(
            [
                (ocean_hbm, ocean_ref),
                (sea_hbm, sea_ref),
                (src_hbm, src_ref),
                (points_hbm, points_ref),
                (emit_hbm, emit_ref),
                (settle_hbm, settle_ref),
                (mass_hbm, mass_ref),
                (kdiff_hbm, kdiff_ref),
                (conc_hbm, conc_ref),
                (wind_hbm, wind_ref),
                (weights_hbm, weights_ref),
                (twiddle_hbm, twiddle_ref),
                (table_hbm, table_ref),
            ]
        )
    ]
    emit_load, settle_load, mass_load, kdiff_load, conc_load, wind_load, weights_load, *tables = rest
    for load in (ocean_load, sea_load, src_load, points_load, *rest):
        load.start()

    ocean_load.wait()
    sea_load.wait()
    own_slot = sec * 6 + 2
    ocean = ocean_ref[...].astype(jnp.float32)
    for block in range(2):
        near_ref[own_slot + block] = jnp.zeros((8, 128), jnp.float32)
        sea = sea_ref[0, block].astype(jnp.float32)
        near_ref[own_slot + block, 0:4, :] = ocean[:, block, :] * sea

    pl.semaphore_wait(barrier, TILES - 1 + 3)

    near_copies = []
    index = 0
    for same_sec in (True, False):
        for shift in (-1, 0, 1):
            if same_sec and shift == 0:
                continue
            peer = lax.rem(lon + shift + TILES, TILES)
            to_sec = sec if same_sec else 1 - sec
            copy = pltpu.make_async_remote_copy(
                src_ref=near_ref.at[pl.ds(own_slot, 2)],
                dst_ref=near_ref.at[pl.ds(sec * 6 + (1 - shift) * 2, 2)],
                send_sem=near_send.at[index],
                recv_sem=near_recv.at[index],
                device_id=(to_sec, lat, peer),
                device_id_type=MESH,
            )
            copy.start()
            near_copies.append(copy)
            index += 1

    kdiff_load.wait()
    conc_load.wait()

    def eliminate(level, carried):
        ratio_prev, scaled_prev = carried
        here = kdiff_ref[level]
        below = kdiff_ref[level + 1]
        inverse = 1.0 / (1.0 + here + below - here * ratio_prev)
        ratio_now = below * inverse
        ratio_ref[level] = ratio_now
        scaled_now = []
        for b in range(NBD):
            value = (conc_ref[level, b].astype(jnp.float32) + here * scaled_prev[b]) * inverse
            scaled_ref[level, b] = value
            scaled_now.append(value)
        return ratio_now, tuple(scaled_now)

    zero = jnp.zeros((ROWS, PTS), jnp.float32)
    ratio_last, scaled_last = lax.fori_loop(0, LEV - 1, eliminate, (zero, (zero,) * NBD))

    row_ids = lax.broadcasted_iota(jnp.int32, (ROWS, PTS), 0)
    columns = lax.broadcasted_iota(jnp.int32, (ROWS, PTS), 1) + lon * PTS
    points_load.wait()
    limits = jnp.zeros((ROWS, PTS), jnp.int32)
    for r in range(ROWS):
        limits = jnp.where(row_ids == r, points_ref[r], limits)
    valid = (columns < limits).astype(jnp.float32)

    for load in (src_load, emit_load, settle_load, mass_load, wind_load, weights_load):
        load.wait()
    for copy in near_copies:
        copy.wait()

    for r in range(ROWS):
        for s in range(4):
            lhs_ref[r, :, s * 128 : (s + 1) * 128] = near_ref[src_ref[0, s, r]]
    for r in range(ROWS):
        fields_ref[r] = jnp.dot(
            lhs_ref[r].astype(jnp.bfloat16),
            weights_ref[r].reshape(512, PTS),
            preferred_element_type=jnp.float32,
        )
    temp = fields_ref[:, 0, :]
    ice = fields_ref[:, 1, :]
    rel_east = wind_ref[0] - 0.5 * fields_ref[:, 2, :]
    rel_north = wind_ref[1] - 0.5 * fields_ref[:, 3, :]
    speed = jnp.sqrt(rel_east * rel_east + rel_north * rel_north + 0.25)
    base = (
        (1.0 - jax.nn.sigmoid(ice))
        * jnp.exp(3.41 * jnp.log(speed))
        * (0.5 + jax.nn.sigmoid(temp))
        * valid
    )

    last_kdiff = kdiff_ref[LEV - 1]
    pivot_part = 1.0 + last_kdiff - last_kdiff * ratio_last
    partial = zero
    for b in range(NBD):
        flux = emit_ref[b] * base
        settle = settle_ref[b]
        value = (
            conc_ref[LEV - 1, b].astype(jnp.float32) + flux + last_kdiff * scaled_last[b]
        ) / (pivot_part + settle)
        scaled_ref[LEV - 1, b] = value
        partial = partial + mass_ref[b] * (flux - settle * value)
    part_ref[...] = partial

    salt_copy = pltpu.make_async_remote_copy(
        src_ref=part_ref,
        dst_ref=other_ref,
        send_sem=salt_send,
        recv_sem=salt_recv,
        device_id=(1 - sec, lat, lon),
        device_id_type=MESH,
    )

    def a2a_copy(chunk, step):
        peer = lax.rem(lon + step, TILES)
        bins = pl.ds(chunk * CHUNK, CHUNK)
        return pltpu.make_async_remote_copy(
            src_ref=out_ref.at[pl.ds(peer * 2, 2), bins],
            dst_ref=recv_ref.at[lon, :, bins],
            send_sem=a2a_send.at[chunk, step],
            recv_sem=a2a_recv.at[chunk, step],
            device_id=(sec, lat, peer),
            device_id_type=MESH,
        )

    def own_copy(chunk):
        bins = pl.ds(chunk * CHUNK, CHUNK)
        return pltpu.make_async_copy(
            out_ref.at[pl.ds(lon * 2, 2), bins], recv_ref.at[lon, :, bins], own_sem.at[chunk]
        )

    keep = valid > 0.0

    @pl.loop(0, NCHUNK)
    def _(chunk):
        first = chunk * CHUNK
        start = tuple(scaled_ref[LEV - 1, first + b] for b in range(CHUNK))
        for b in range(CHUNK):
            out_ref[LEV - 1, first + b] = jnp.where(keep, start[b], 0.0).astype(jnp.bfloat16)

        def substitute(count, carried):
            level = LEV - 2 - count
            ratio = ratio_ref[level]
            values = []
            for b in range(CHUNK):
                value = scaled_ref[level, first + b] + ratio * carried[b]
                out_ref[level, first + b] = jnp.where(keep, value, 0.0).astype(jnp.bfloat16)
                values.append(value)
            return tuple(values)

        lax.fori_loop(0, LEV - 1, substitute, start)

        @pl.when(chunk == 0)
        def _():
            salt_copy.start()

        for step in ORDER:
            a2a_copy(chunk, step).start()
        own_copy(chunk).start()

    for load in tables:
        load.wait()
    salt_copy.wait()
    salt_ref[...] = (part_ref[...] + other_ref[...]) * valid

    def y_copy(chunk, part):
        return pltpu.make_async_copy(
            y_ref.at[part], spectra_hbm.at[part, pl.ds(chunk * CHUNK, CHUNK)], y_sem.at[part]
        )

    @pl.loop(0, NCHUNK)
    def _(chunk):
        own_copy(chunk).wait()
        for step in ORDER:
            a2a_copy(chunk, step).wait()
        for part in range(2):

            @pl.when(chunk > 0)
            def _():
                y_copy(chunk - 1, part).wait()

            transform(
                recv_ref.at[:, part, pl.ds(chunk * CHUNK, CHUNK)],
                twiddle_ref,
                table_ref,
                y_ref.at[part],
                z_ref,
                o_ref,
            )
            y_copy(chunk, part).start()

    for part in range(2):
        y_copy(NCHUNK - 1, part).wait()


def fused(*operands):
    vmem = pl.BlockSpec(memory_space=pltpu.VMEM)
    anywhere = pl.BlockSpec(memory_space=pl.ANY)
    dma = pltpu.SemaphoreType.DMA
    return pl.pallas_call(
        fused_kernel,
        name="fused",
        out_shape=(
            jax.ShapeDtypeStruct((2, NBD, ROWS, 2, K), jnp.float32),
            jax.ShapeDtypeStruct((ROWS, PTS), jnp.float32),
        ),
        in_specs=[anywhere] * 13,
        out_specs=(anywhere, vmem),
        scratch_shapes=[
            pltpu.VMEM((4, 2, 128), jnp.bfloat16),
            pltpu.SMEM((1, 2), jnp.int32),
            pltpu.SMEM((1, 4, 8), jnp.int32),
            pltpu.SMEM((ROWS,), jnp.int32),
            pltpu.SMEM((NBD,), jnp.float32),
            pltpu.SMEM((NBD,), jnp.float32),
            pltpu.SMEM((NBD,), jnp.float32),
            pltpu.VMEM((2, ROWS, PTS), jnp.float32),
            pltpu.VMEM((ROWS, 4, 128, PTS), jnp.bfloat16),
            pltpu.VMEM((LEV, NBD, ROWS, PTS), jnp.bfloat16),
            pltpu.VMEM((LEV, ROWS, PTS), jnp.float32),
            pltpu.VMEM((TILES, 2, PTS), jnp.float32),
            pltpu.VMEM((4 * PTS, 256), jnp.bfloat16),
            pltpu.VMEM((12, 8, 128), jnp.float32),
            pltpu.VMEM((ROWS, 8, 512), jnp.float32),
            pltpu.VMEM((ROWS, 8, PTS), jnp.float32),
            pltpu.VMEM((LEV, ROWS, PTS), jnp.float32),
            pltpu.VMEM((LEV, NBD, ROWS, PTS), jnp.float32),
            pltpu.VMEM((LEV, NBD, ROWS, PTS), jnp.bfloat16),
            pltpu.VMEM((TILES, 2, NBD, ROWS, PTS), jnp.bfloat16),
            pltpu.VMEM((ROWS, PTS), jnp.float32),
            pltpu.VMEM((ROWS, PTS), jnp.float32),
            pltpu.VMEM((TILES, 16, 4 * PTS), jnp.bfloat16),
            pltpu.VMEM((TILES, 16, 256), jnp.float32),
            pltpu.VMEM((2, CHUNK, ROWS, 2, K), jnp.float32),
            dma((13,)),
            dma((NCHUNK,)),
            dma((5,)),
            dma((5,)),
            dma,
            dma,
            dma((NCHUNK, TILES)),
            dma((NCHUNK, TILES)),
            dma((2,)),
        ],
        compiler_params=pltpu.CompilerParams(collective_id=0, has_side_effects=True),
    )(*operands)


def twiddles():
    phase = np.arange(TILES)[:, None] * np.arange(PTS)[None, :] * (2.0 * np.pi / M)
    parts = np.stack([np.cos(phase), np.sin(phase)], axis=1) * (1.0 / math.sqrt(M))
    return parts.astype(np.float32)


def row_table():
    column = np.arange(256)
    combo = (column // 128) * 16 + column % 16
    ka = 8 * (combo // 2) + (column % 128) // 16
    phase = np.arange(PTS)[:, None] * ka[None, :] % PTS * (2.0 * np.pi / PTS)
    cos, sin = np.cos(phase), np.sin(phase)
    is_cos = (combo % 2 == 0)[None, :]
    upper = np.where(is_cos, cos, -sin)
    lower = np.where(is_cos, -sin, -cos)
    table = np.concatenate([upper, lower], axis=0) * (combo < 20)[None, :]
    return table.astype(np.float32)


def real_dft16(x):
    c1, c2, c3 = math.cos(math.pi / 8), math.cos(math.pi / 4), math.cos(3 * math.pi / 8)
    s = [x[i] + x[i + 8] for i in range(8)]
    d = [x[i] - x[i + 8] for i in range(8)]
    a = [s[i] + s[i + 4] for i in range(4)]
    b = [s[i] - s[i + 4] for i in range(4)]
    out = [None] * 9
    a02, a13 = a[0] + a[2], a[1] + a[3]
    out[0] = (a02 + a13, None)
    out[8] = (a02 - a13, None)
    out[4] = (a[0] - a[2], a[1] - a[3])
    bm, bp = (b[1] - b[3]) * c2, (b[1] + b[3]) * c2
    out[2] = (b[0] + bm, bp + b[2])
    out[6] = (b[0] - bm, bp - b[2])
    e1, e2, e3 = d[1] - d[7], (d[2] - d[6]) * c2, d[3] - d[5]
    f1, f2, f3 = d[1] + d[7], (d[2] + d[6]) * c2, d[3] + d[5]
    p, q = d[0] + e2, d[0] - e2
    u, v = e1 * c1 + e3 * c3, e1 * c3 - e3 * c1
    g, h = f1 * c3 + f3 * c1, f1 * c1 - f3 * c3
    m, n = f2 + d[4], f2 - d[4]
    out[1] = (p + u, g + m)
    out[7] = (p - u, g - m)
    out[3] = (q + v, h + n)
    out[5] = (q - v, h - n)
    return out


def transform(x_ref, twiddle_ref, table_ref, y_ref, z_ref, o_ref):
    for half in range(2):
        lanes = slice(half * 128, (half + 1) * 128)
        x = [
            x_ref[tile, :, :, lanes].astype(jnp.float32).reshape(16, 128)
            for tile in range(TILES)
        ]
        coefficients = real_dft16(x)
        for kb in range(TILES):
            re, im = coefficients[min(kb, TILES - kb)]
            cos = twiddle_ref[kb, 0:1, lanes]
            sin = twiddle_ref[kb, 1:2, lanes]
            if im is None:
                real, minus = re * cos, re * sin
            elif kb < 8:
                real, minus = re * cos - im * sin, re * sin + im * cos
            else:
                real, minus = re * cos + im * sin, re * sin - im * cos
            for part, value in enumerate((real, minus)):
                high = value.astype(jnp.bfloat16)
                low = (value - high.astype(jnp.float32)).astype(jnp.bfloat16)
                at = part * PTS + half * 128
                z_ref[kb, :, at : at + 128] = high
                z_ref[kb, :, 2 * PTS + at : 2 * PTS + at + 128] = low
    o_ref[...] = jnp.dot(
        z_ref[...].reshape(TILES * 16, 4 * PTS), table_ref[...], preferred_element_type=jnp.float32
    ).reshape(TILES, 16, 256)
    lane = lax.broadcasted_iota(jnp.int32, (8, 128), 1)
    for group in range(2):
        for q in range(2):
            combos = 16 if q == 0 else 4
            arrays = {
                kb: pltpu.roll(
                    o_ref[kb, group * 8 : (group + 1) * 8, q * 128 : (q + 1) * 128], kb, axis=1
                )
                for kb in range(TILES)
            }
            wanted = {(-t) % TILES for t in range(combos)}
            needs = [wanted]
            for bit in (0, 1, 2):
                wanted = wanted | {(j + (1 << bit)) % TILES for j in wanted}
                needs.append(wanted)
            for bit in (3, 2, 1, 0):
                taken = (lane & (1 << bit)) != 0
                arrays = {
                    j: jnp.where(taken, arrays[(j + (1 << bit)) % TILES], arrays[j])
                    for j in needs[bit]
                }
            for t in range(combos):
                value = arrays[(-t) % TILES]
                if t:
                    value = pltpu.roll(value, 128 - t, axis=1)
                c, part = divmod(q * 16 + t, 2)
                y_ref[group, :, part, c * 128 : (c + 1) * 128] = value


def on_device(
    ocean_state,
    sea_tiles,
    regrid_weights,
    regrid_src,
    row_points,
    wind,
    conc,
    kdiff,
    bin_emit,
    bin_settle,
    bin_mass,
):
    table = jnp.asarray(row_table()).astype(jnp.bfloat16)
    return fused(
        ocean_state.reshape(4, 2, 128),
        sea_tiles.reshape(1, 2),
        jnp.transpose(regrid_src, (1, 2, 0)),
        row_points,
        bin_emit,
        bin_settle,
        bin_mass,
        wind,
        regrid_weights,
        conc,
        kdiff,
        jnp.asarray(twiddles()),
        jnp.concatenate([table, table], axis=0),
    )


def solution(mesh):
    return jax.shard_map(
        on_device,
        mesh=mesh,
        in_specs=(
            P(None, "sec", "lat", "lon", None),
            P("sec", "lat", "lon"),
            P("lat", None, None, "lon"),
            P("lat", "lon", None),
            P("lat"),
            P(None, "lat", "lon"),
            P(None, "sec", "lat", "lon"),
            P(None, "lat", "lon"),
            P("sec"),
            P("sec"),
            P("sec"),
        ),
        out_specs=(P("lon", "sec", "lat", None, None), P("lat", "lon")),
        check_vma=False,
    )
```

```python
import functools
import math

import jax
import jax.numpy as jnp
import numpy as np
from jax import lax
from jax.experimental import pallas as pl
from jax.experimental.pallas import tpu as pltpu
from jax.sharding import PartitionSpec as P

M = 4096
K = 1280
LEV = 32
TILES = 16
PTS = 256
NBD = 10
ROWS = 8
ORDER = (10, 9, 11, 8, 6, 14, 5, 13, 7, 15, 4, 12, 2, 1, 3)
MESH = pl.DeviceIdType.MESH


def peer_of(lon, step):
    z = lax.rem(lon // 4 + step // 4, 4)
    x = lax.rem(lon % 4 + step % 4, 4)
    return z * 4 + x


def far(step):
    return step // 4 == 2 and step % 4 != 0


def fused_kernel(
    ocean_hbm,
    sea_hbm,
    src_hbm,
    points_hbm,
    emit_hbm,
    settle_hbm,
    mass_hbm,
    wind_hbm,
    weights_hbm,
    conc_hbm,
    kdiff_hbm,
    twiddle_hbm,
    table_hbm,
    spectra_ref,
    salt_ref,
    ocean_ref,
    sea_ref,
    src_ref,
    points_ref,
    emit_ref,
    settle_ref,
    mass_ref,
    wind_ref,
    weights_ref,
    conc_ref,
    kdiff_ref,
    twiddle_ref,
    table_ref,
    near_ref,
    lhs_ref,
    fields_ref,
    ratio_ref,
    scaled_ref,
    out_ref,
    recv_ref,
    part_ref,
    other_ref,
    z_ref,
    o_ref,
    local_sem,
    own_sem,
    near_send,
    near_recv,
    salt_send,
    salt_recv,
    a2a_send,
    a2a_recv,
    row_sem,
):
    sec = lax.axis_index("sec")
    lat = lax.axis_index("lat")
    lon = lax.axis_index("lon")

    barrier = pltpu.get_barrier_semaphore()
    greeted = 3
    for step in range(1, TILES):
        if far(step):
            continue
        peer = peer_of(lon, step)
        pl.semaphore_signal(barrier, inc=1, device_id=(sec, lat, peer), device_id_type=MESH)
        greeted += 1
    for shift in (-1, 0, 1):
        peer = lax.rem(lon + shift + TILES, TILES)
        pl.semaphore_signal(barrier, inc=1, device_id=(1 - sec, lat, peer), device_id_type=MESH)

    ocean_load, sea_load, src_load, points_load, *rest = [
        pltpu.make_async_copy(source, target, local_sem.at[i])
        for i, (source, target) in enumerate(
            [
                (ocean_hbm, ocean_ref),
                (sea_hbm, sea_ref),
                (src_hbm, src_ref),
                (points_hbm, points_ref),
                (emit_hbm, emit_ref),
                (settle_hbm, settle_ref),
                (mass_hbm, mass_ref),
                (kdiff_hbm, kdiff_ref),
                (conc_hbm, conc_ref),
                (wind_hbm, wind_ref),
                (weights_hbm, weights_ref),
                (twiddle_hbm, twiddle_ref),
                (table_hbm, table_ref),
            ]
        )
    ]
    emit_load, settle_load, mass_load, kdiff_load, conc_load, wind_load, weights_load, *tables = rest
    for load in (ocean_load, sea_load, src_load, points_load, *rest):
        load.start()

    ocean_load.wait()
    sea_load.wait()
    own_slot = sec * 6 + 2
    ocean = ocean_ref[...].astype(jnp.float32)
    for block in range(2):
        near_ref[own_slot + block] = jnp.zeros((8, 128), jnp.float32)
        sea = sea_ref[0, block].astype(jnp.float32)
        near_ref[own_slot + block, 0:4, :] = ocean[:, block, :] * sea

    pl.semaphore_wait(barrier, greeted)
    pl.semaphore_signal(
        row_sem, inc=1, device_id=(sec, lat, peer_of(lon, 8)), device_id_type=MESH
    )

    near_copies = []
    index = 0
    for same_sec in (True, False):
        for shift in (-1, 0, 1):
            if same_sec and shift == 0:
                continue
            peer = lax.rem(lon + shift + TILES, TILES)
            to_sec = sec if same_sec else 1 - sec
            copy = pltpu.make_async_remote_copy(
                src_ref=near_ref.at[pl.ds(own_slot, 2)],
                dst_ref=near_ref.at[pl.ds(sec * 6 + (1 - shift) * 2, 2)],
                send_sem=near_send.at[index],
                recv_sem=near_recv.at[index],
                device_id=(to_sec, lat, peer),
                device_id_type=MESH,
            )
            copy.start()
            near_copies.append(copy)
            index += 1

    kdiff_load.wait()
    conc_load.wait()

    def eliminate(level, carried):
        ratio_prev, scaled_prev = carried
        here = kdiff_ref[level]
        below = kdiff_ref[level + 1]
        inverse = 1.0 / (1.0 + here + below - here * ratio_prev)
        ratio_now = below * inverse
        ratio_ref[level] = ratio_now
        scaled_now = []
        for b in range(NBD):
            value = (conc_ref[level, b].astype(jnp.float32) + here * scaled_prev[b]) * inverse
            scaled_ref[level, b] = value
            scaled_now.append(value)
        return ratio_now, tuple(scaled_now)

    zero = jnp.zeros((ROWS, PTS), jnp.float32)
    ratio_last, scaled_last = lax.fori_loop(0, LEV - 1, eliminate, (zero, (zero,) * NBD))

    row_ids = lax.broadcasted_iota(jnp.int32, (ROWS, PTS), 0)
    columns = lax.broadcasted_iota(jnp.int32, (ROWS, PTS), 1) + lon * PTS
    points_load.wait()
    limits = jnp.zeros((ROWS, PTS), jnp.int32)
    for r in range(ROWS):
        limits = jnp.where(row_ids == r, points_ref[r], limits)
    valid = (columns < limits).astype(jnp.float32)

    for load in (src_load, emit_load, settle_load, mass_load, wind_load, weights_load):
        load.wait()
    for copy in near_copies:
        copy.wait()

    for r in range(ROWS):
        for s in range(4):
            lhs_ref[r, :, s * 128 : (s + 1) * 128] = near_ref[src_ref[0, s, r]]
    for r in range(ROWS):
        fields_ref[r] = jnp.dot(
            lhs_ref[r].astype(jnp.bfloat16),
            weights_ref[r].reshape(512, PTS),
            preferred_element_type=jnp.float32,
        )
    temp = fields_ref[:, 0, :]
    ice = fields_ref[:, 1, :]
    rel_east = wind_ref[0] - 0.5 * fields_ref[:, 2, :]
    rel_north = wind_ref[1] - 0.5 * fields_ref[:, 3, :]
    speed = jnp.sqrt(rel_east * rel_east + rel_north * rel_north + 0.25)
    base = (
        (1.0 - jax.nn.sigmoid(ice))
        * jnp.exp(3.41 * jnp.log(speed))
        * (0.5 + jax.nn.sigmoid(temp))
        * valid
    )

    last_kdiff = kdiff_ref[LEV - 1]
    pivot_part = 1.0 + last_kdiff - last_kdiff * ratio_last
    partial = zero
    for b in range(NBD):
        flux = emit_ref[b] * base
        settle = settle_ref[b]
        value = (
            conc_ref[LEV - 1, b].astype(jnp.float32) + flux + last_kdiff * scaled_last[b]
        ) / (pivot_part + settle)
        scaled_ref[LEV - 1, b] = value
        partial = partial + mass_ref[b] * (flux - settle * value)
    part_ref[...] = partial

    salt_copy = pltpu.make_async_remote_copy(
        src_ref=part_ref,
        dst_ref=other_ref,
        send_sem=salt_send,
        recv_sem=salt_recv,
        device_id=(1 - sec, lat, lon),
        device_id_type=MESH,
    )

    def a2a_copy(b, step):
        peer = peer_of(lon, step)
        return pltpu.make_async_remote_copy(
            src_ref=out_ref.at[pl.ds(peer * 2, 2), b],
            dst_ref=recv_ref.at[lon, :, b],
            send_sem=a2a_send.at[b, step],
            recv_sem=a2a_recv.at[b, step],
            device_id=(sec, lat, peer),
            device_id_type=MESH,
        )

    def own_copy(b):
        return pltpu.make_async_copy(
            out_ref.at[pl.ds(lon * 2, 2), b], recv_ref.at[lon, :, b], own_sem.at[b]
        )

    keep = valid > 0.0
    pl.semaphore_wait(row_sem, 1)

    @pl.loop(0, NBD)
    def _(b):
        start = scaled_ref[LEV - 1, b]
        out_ref[LEV - 1, b] = jnp.where(keep, start, 0.0).astype(jnp.bfloat16)

        def substitute(count, below):
            level = LEV - 2 - count
            value = scaled_ref[level, b] + ratio_ref[level] * below
            out_ref[level, b] = jnp.where(keep, value, 0.0).astype(jnp.bfloat16)
            return value

        lax.fori_loop(0, LEV - 1, substitute, start)

        @pl.when(b == 0)
        def _():
            salt_copy.start()

        for step in ORDER:
            a2a_copy(b, step).start()
        own_copy(b).start()

    for load in tables:
        load.wait()
    salt_copy.wait()
    salt_ref[...] = (part_ref[...] + other_ref[...]) * valid

    @pl.loop(0, NBD)
    def _(b):
        own_copy(b).wait()
        for step in ORDER:
            a2a_copy(b, step).wait()
        transform(recv_ref.at[:, :, b], twiddle_ref, table_ref, spectra_ref.at[:, b], z_ref, o_ref)


def deliver_kernel(from_spectra, from_salt, to_spectra, to_salt, sems):
    copies = [
        pltpu.make_async_copy(
            from_spectra.at[part, pl.ds(5 * i, 5)], to_spectra.at[part, pl.ds(5 * i, 5)], sems.at[2 * part + i]
        )
        for part in range(2)
        for i in range(2)
    ]
    copies.append(pltpu.make_async_copy(from_salt, to_salt, sems.at[4]))
    for copy in copies:
        copy.start()
    for copy in copies:
        copy.wait()


def deliver(spectra, salt):
    anywhere = pl.BlockSpec(memory_space=pl.ANY)
    vmem = pl.BlockSpec(memory_space=pltpu.VMEM)
    return pl.pallas_call(
        deliver_kernel,
        name="deliver",
        out_shape=tuple(jax.ShapeDtypeStruct(a.shape, a.dtype) for a in (spectra, salt)),
        in_specs=[anywhere] * 2,
        out_specs=(anywhere, anywhere),
        scratch_shapes=[pltpu.SemaphoreType.DMA((5,))],
        compiler_params=pltpu.CompilerParams(vmem_limit_bytes=2**20),
    )(spectra, salt)


def fused(*operands):
    vmem = pl.BlockSpec(memory_space=pltpu.VMEM)
    anywhere = pl.BlockSpec(memory_space=pl.ANY)
    dma = pltpu.SemaphoreType.DMA
    return pl.pallas_call(
        fused_kernel,
        name="fused",
        out_shape=(
            jax.ShapeDtypeStruct((2, NBD, ROWS, 2, K), jnp.float32),
            jax.ShapeDtypeStruct((ROWS, PTS), jnp.float32),
        ),
        in_specs=[pl.BlockSpec(memory_space=pltpu.HBM)] * 13,
        out_specs=(vmem, vmem),
        scratch_shapes=[
            pltpu.VMEM((4, 2, 128), jnp.bfloat16),
            pltpu.SMEM((1, 2), jnp.int32),
            pltpu.SMEM((1, 4, 8), jnp.int32),
            pltpu.SMEM((ROWS,), jnp.int32),
            pltpu.SMEM((NBD,), jnp.float32),
            pltpu.SMEM((NBD,), jnp.float32),
            pltpu.SMEM((NBD,), jnp.float32),
            pltpu.VMEM((2, ROWS, PTS), jnp.float32),
            pltpu.VMEM((ROWS, 4, 128, PTS), jnp.bfloat16),
            pltpu.VMEM((LEV, NBD, ROWS, PTS), jnp.bfloat16),
            pltpu.VMEM((LEV, ROWS, PTS), jnp.float32),
            pltpu.VMEM((TILES, 2, PTS), jnp.float32),
            pltpu.VMEM((4 * PTS, 256), jnp.bfloat16),
            pltpu.VMEM((12, 8, 128), jnp.float32),
            pltpu.VMEM((ROWS, 8, 512), jnp.float32),
            pltpu.VMEM((ROWS, 8, PTS), jnp.float32),
            pltpu.VMEM((LEV, ROWS, PTS), jnp.float32),
            pltpu.VMEM((LEV, NBD, ROWS, PTS), jnp.float32),
            pltpu.VMEM((LEV, NBD, ROWS, PTS), jnp.bfloat16),
            pltpu.VMEM((TILES, 2, NBD, ROWS, PTS), jnp.bfloat16),
            pltpu.VMEM((ROWS, PTS), jnp.float32),
            pltpu.VMEM((ROWS, PTS), jnp.float32),
            pltpu.VMEM((TILES, 16, 4 * PTS), jnp.bfloat16),
            pltpu.VMEM((TILES, 16, 256), jnp.float32),
            dma((13,)),
            dma((NBD,)),
            dma((5,)),
            dma((5,)),
            dma,
            dma,
            dma((NBD, TILES)),
            dma((NBD, TILES)),
            pltpu.SemaphoreType.REGULAR,
        ],
        compiler_params=pltpu.CompilerParams(
            collective_id=0, has_side_effects=True, vmem_limit_bytes=16 * 2**20
        ),
    )(*[pltpu.with_memory_space_constraint(a, pltpu.HBM) for a in operands])


def twiddles():
    phase = np.arange(TILES)[:, None] * np.arange(PTS)[None, :] * (2.0 * np.pi / M)
    parts = np.stack([np.cos(phase), np.sin(phase)], axis=1) * (1.0 / math.sqrt(M))
    return parts.astype(np.float32)


def row_table():
    column = np.arange(256)
    combo = (column // 128) * 16 + column % 16
    ka = 8 * (combo // 2) + (column % 128) // 16
    phase = np.arange(PTS)[:, None] * ka[None, :] % PTS * (2.0 * np.pi / PTS)
    cos, sin = np.cos(phase), np.sin(phase)
    is_cos = (combo % 2 == 0)[None, :]
    upper = np.where(is_cos, cos, -sin)
    lower = np.where(is_cos, -sin, -cos)
    table = np.concatenate([upper, lower], axis=0) * (combo < 20)[None, :]
    return table.astype(np.float32)


def real_dft16(x):
    c1, c2, c3 = math.cos(math.pi / 8), math.cos(math.pi / 4), math.cos(3 * math.pi / 8)
    s = [x[i] + x[i + 8] for i in range(8)]
    d = [x[i] - x[i + 8] for i in range(8)]
    a = [s[i] + s[i + 4] for i in range(4)]
    b = [s[i] - s[i + 4] for i in range(4)]
    out = [None] * 9
    a02, a13 = a[0] + a[2], a[1] + a[3]
    out[0] = (a02 + a13, None)
    out[8] = (a02 - a13, None)
    out[4] = (a[0] - a[2], a[1] - a[3])
    bm, bp = (b[1] - b[3]) * c2, (b[1] + b[3]) * c2
    out[2] = (b[0] + bm, bp + b[2])
    out[6] = (b[0] - bm, bp - b[2])
    e1, e2, e3 = d[1] - d[7], (d[2] - d[6]) * c2, d[3] - d[5]
    f1, f2, f3 = d[1] + d[7], (d[2] + d[6]) * c2, d[3] + d[5]
    p, q = d[0] + e2, d[0] - e2
    u, v = e1 * c1 + e3 * c3, e1 * c3 - e3 * c1
    g, h = f1 * c3 + f3 * c1, f1 * c1 - f3 * c3
    m, n = f2 + d[4], f2 - d[4]
    out[1] = (p + u, g + m)
    out[7] = (p - u, g - m)
    out[3] = (q + v, h + n)
    out[5] = (q - v, h - n)
    return out


def transform(x_ref, twiddle_ref, table_ref, y_ref, z_ref, o_ref):
    for half in range(2):
        lanes = slice(half * 128, (half + 1) * 128)
        x = [
            x_ref[tile, :, :, lanes].astype(jnp.float32).reshape(16, 128)
            for tile in range(TILES)
        ]
        coefficients = real_dft16(x)
        for kb in range(TILES):
            re, im = coefficients[min(kb, TILES - kb)]
            cos = twiddle_ref[kb, 0:1, lanes]
            sin = twiddle_ref[kb, 1:2, lanes]
            if im is None:
                real, minus = re * cos, re * sin
            elif kb < 8:
                real, minus = re * cos - im * sin, re * sin + im * cos
            else:
                real, minus = re * cos + im * sin, re * sin - im * cos
            for part, value in enumerate((real, minus)):
                high = value.astype(jnp.bfloat16)
                low = (value - high.astype(jnp.float32)).astype(jnp.bfloat16)
                at = part * PTS + half * 128
                z_ref[kb, :, at : at + 128] = high
                z_ref[kb, :, 2 * PTS + at : 2 * PTS + at + 128] = low
    o_ref[...] = jnp.dot(
        z_ref[...].reshape(TILES * 16, 4 * PTS), table_ref[...], preferred_element_type=jnp.float32
    ).reshape(TILES, 16, 256)
    lane = lax.broadcasted_iota(jnp.int32, (8, 128), 1)
    for group in range(2):
        for q in range(2):
            combos = 16 if q == 0 else 4
            arrays = {
                kb: pltpu.roll(
                    o_ref[kb, group * 8 : (group + 1) * 8, q * 128 : (q + 1) * 128], kb, axis=1
                )
                for kb in range(TILES)
            }
            wanted = {(-t) % TILES for t in range(combos)}
            needs = [wanted]
            for bit in (0, 1, 2):
                wanted = wanted | {(j + (1 << bit)) % TILES for j in wanted}
                needs.append(wanted)
            for bit in (3, 2, 1, 0):
                taken = (lane & (1 << bit)) != 0
                arrays = {
                    j: jnp.where(taken, arrays[(j + (1 << bit)) % TILES], arrays[j])
                    for j in needs[bit]
                }
            for t in range(combos):
                value = arrays[(-t) % TILES]
                if t:
                    value = pltpu.roll(value, 128 - t, axis=1)
                c, part = divmod(q * 16 + t, 2)
                y_ref[group, :, part, c * 128 : (c + 1) * 128] = value


def on_device(
    ocean_state,
    sea_tiles,
    regrid_weights,
    regrid_src,
    row_points,
    wind,
    conc,
    kdiff,
    bin_emit,
    bin_settle,
    bin_mass,
):
    table = jnp.asarray(row_table()).astype(jnp.bfloat16)
    spectra, salt = fused(
        ocean_state.reshape(4, 2, 128),
        sea_tiles.reshape(1, 2),
        jnp.transpose(regrid_src, (1, 2, 0)),
        row_points,
        bin_emit,
        bin_settle,
        bin_mass,
        wind,
        regrid_weights,
        conc,
        kdiff,
        jnp.asarray(twiddles()),
        jnp.concatenate([table, table], axis=0),
    )
    return deliver(spectra, salt)


def solution(mesh):
    return jax.shard_map(
        on_device,
        mesh=mesh,
        in_specs=(
            P(None, "sec", "lat", "lon", None),
            P("sec", "lat", "lon"),
            P("lat", None, None, "lon"),
            P("lat", "lon", None),
            P("lat"),
            P(None, "lat", "lon"),
            P(None, "sec", "lat", "lon"),
            P(None, "lat", "lon"),
            P("sec"),
            P("sec"),
            P("sec"),
        ),
        out_specs=(P("lon", "sec", "lat", None, None), P("lat", "lon")),
        check_vma=False,
    )
```

```python
import functools
import math

import jax
import jax.numpy as jnp
import numpy as np
from jax import lax
from jax.experimental import pallas as pl
from jax.experimental.pallas import tpu as pltpu
from jax.sharding import PartitionSpec as P

M = 4096
K = 1280
LEV = 32
TILES = 16
PTS = 256
NBD = 10
ROWS = 8
ORDER = (10, 9, 11, 8, 6, 14, 5, 13, 7, 15, 4, 12, 2, 1, 3)
MESH = pl.DeviceIdType.MESH


def peer_of(lon, step):
    z = lax.rem(lon // 4 + step // 4, 4)
    x = lax.rem(lon % 4 + step % 4, 4)
    return z * 4 + x


def far(step):
    return step // 4 == 2 and step % 4 != 0


def fused_kernel(
    ocean_hbm,
    sea_hbm,
    src_hbm,
    points_hbm,
    emit_hbm,
    settle_hbm,
    mass_hbm,
    wind_hbm,
    weights_hbm,
    conc_hbm,
    kdiff_hbm,
    twiddle_hbm,
    table_hbm,
    spectra_ref,
    salt_ref,
    ocean_ref,
    sea_ref,
    src_ref,
    points_ref,
    emit_ref,
    settle_ref,
    mass_ref,
    wind_ref,
    weights_ref,
    conc_ref,
    kdiff_ref,
    twiddle_ref,
    table_ref,
    near_ref,
    lhs_ref,
    fields_ref,
    ratio_ref,
    scaled_ref,
    out_ref,
    recv_ref,
    part_ref,
    other_ref,
    z_ref,
    o_ref,
    local_sem,
    near_send,
    near_recv,
    salt_send,
    salt_recv,
    a2a_send,
    a2a_recv,
    row_sem,
):
    sec = lax.axis_index("sec")
    lat = lax.axis_index("lat")
    lon = lax.axis_index("lon")

    barrier = pltpu.get_barrier_semaphore()
    greeted = 3
    for step in range(1, TILES):
        if far(step):
            continue
        peer = peer_of(lon, step)
        pl.semaphore_signal(barrier, inc=1, device_id=(sec, lat, peer), device_id_type=MESH)
        greeted += 1
    for shift in (-1, 0, 1):
        peer = lax.rem(lon + shift + TILES, TILES)
        pl.semaphore_signal(barrier, inc=1, device_id=(1 - sec, lat, peer), device_id_type=MESH)

    ocean_load, sea_load, src_load, points_load, *rest = [
        pltpu.make_async_copy(source, target, local_sem.at[i])
        for i, (source, target) in enumerate(
            [
                (ocean_hbm, ocean_ref),
                (sea_hbm, sea_ref),
                (src_hbm, src_ref),
                (points_hbm, points_ref),
                (emit_hbm, emit_ref),
                (settle_hbm, settle_ref),
                (mass_hbm, mass_ref),
                (kdiff_hbm, kdiff_ref),
                (conc_hbm, conc_ref),
                (wind_hbm, wind_ref),
                (weights_hbm, weights_ref),
                (twiddle_hbm, twiddle_ref),
                (table_hbm, table_ref),
            ]
        )
    ]
    emit_load, settle_load, mass_load, kdiff_load, conc_load, wind_load, weights_load, *tables = rest
    for load in (ocean_load, sea_load, src_load, points_load, *rest):
        load.start()

    ocean_load.wait()
    sea_load.wait()
    own_slot = sec * 6 + 2
    ocean = ocean_ref[...].astype(jnp.float32)
    for block in range(2):
        near_ref[own_slot + block] = jnp.zeros((8, 128), jnp.float32)
        sea = sea_ref[0, block].astype(jnp.float32)
        near_ref[own_slot + block, 0:4, :] = ocean[:, block, :] * sea

    pl.semaphore_wait(barrier, greeted)
    pl.semaphore_signal(
        row_sem, inc=1, device_id=(sec, lat, peer_of(lon, 8)), device_id_type=MESH
    )

    for same_sec in (True, False):
        for shift in (-1, 0, 1):
            if same_sec and shift == 0:
                continue
            peer = lax.rem(lon + shift + TILES, TILES)
            to_sec = sec if same_sec else 1 - sec
            copy = pltpu.make_async_remote_copy(
                src_ref=near_ref.at[pl.ds(own_slot, 2)],
                dst_ref=near_ref.at[pl.ds(sec * 6 + (1 - shift) * 2, 2)],
                send_sem=near_send,
                recv_sem=near_recv,
                device_id=(to_sec, lat, peer),
                device_id_type=MESH,
            )
            copy.start()

    kdiff_load.wait()
    conc_load.wait()

    def eliminate(level, carried):
        ratio_prev, scaled_prev = carried
        here = kdiff_ref[level]
        below = kdiff_ref[level + 1]
        inverse = 1.0 / (1.0 + here + below - here * ratio_prev)
        ratio_now = below * inverse
        ratio_ref[level] = ratio_now
        scaled_now = []
        for b in range(NBD):
            value = (conc_ref[level, b].astype(jnp.float32) + here * scaled_prev[b]) * inverse
            scaled_ref[level, b] = value
            scaled_now.append(value)
        return ratio_now, tuple(scaled_now)

    zero = jnp.zeros((ROWS, PTS), jnp.float32)
    ratio_last, scaled_last = lax.fori_loop(0, LEV - 1, eliminate, (zero, (zero,) * NBD))

    row_ids = lax.broadcasted_iota(jnp.int32, (ROWS, PTS), 0)
    columns = lax.broadcasted_iota(jnp.int32, (ROWS, PTS), 1) + lon * PTS
    points_load.wait()
    limits = jnp.zeros((ROWS, PTS), jnp.int32)
    for r in range(ROWS):
        limits = jnp.where(row_ids == r, points_ref[r], limits)
    valid = (columns < limits).astype(jnp.float32)

    for load in (src_load, emit_load, settle_load, mass_load, wind_load, weights_load):
        load.wait()
    five = near_ref.at[pl.ds(0, 10)]
    pltpu.make_async_copy(five, five, near_recv).wait()
    pltpu.make_async_copy(five, five, near_send).wait()

    for r in range(ROWS):
        for s in range(4):
            lhs_ref[r, :, s * 128 : (s + 1) * 128] = near_ref[src_ref[0, s, r]]
    for r in range(ROWS):
        fields_ref[r] = jnp.dot(
            lhs_ref[r].astype(jnp.bfloat16),
            weights_ref[r].reshape(512, PTS),
            preferred_element_type=jnp.float32,
        )
    temp = fields_ref[:, 0, :]
    ice = fields_ref[:, 1, :]
    rel_east = wind_ref[0] - 0.5 * fields_ref[:, 2, :]
    rel_north = wind_ref[1] - 0.5 * fields_ref[:, 3, :]
    speed = jnp.sqrt(rel_east * rel_east + rel_north * rel_north + 0.25)
    base = (
        (1.0 - jax.nn.sigmoid(ice))
        * jnp.exp(3.41 * jnp.log(speed))
        * (0.5 + jax.nn.sigmoid(temp))
        * valid
    )

    last_kdiff = kdiff_ref[LEV - 1]
    pivot_part = 1.0 + last_kdiff - last_kdiff * ratio_last
    partial = zero
    for b in range(NBD):
        flux = emit_ref[b] * base
        settle = settle_ref[b]
        value = (
            conc_ref[LEV - 1, b].astype(jnp.float32) + flux + last_kdiff * scaled_last[b]
        ) / (pivot_part + settle)
        scaled_ref[LEV - 1, b] = value
        partial = partial + mass_ref[b] * (flux - settle * value)
    part_ref[...] = partial

    salt_copy = pltpu.make_async_remote_copy(
        src_ref=part_ref,
        dst_ref=other_ref,
        send_sem=salt_send,
        recv_sem=salt_recv,
        device_id=(1 - sec, lat, lon),
        device_id_type=MESH,
    )

    def a2a_copy(b, step):
        peer = peer_of(lon, step)
        return pltpu.make_async_remote_copy(
            src_ref=out_ref.at[pl.ds(peer * 2, 2), b],
            dst_ref=recv_ref.at[lon, :, b],
            send_sem=a2a_send,
            recv_sem=a2a_recv.at[b],
            device_id=(sec, lat, peer),
            device_id_type=MESH,
        )

    def own_copy(b):
        return pltpu.make_async_copy(
            out_ref.at[pl.ds(lon * 2, 2), b], recv_ref.at[lon, :, b], a2a_recv.at[b]
        )

    keep = valid > 0.0
    pl.semaphore_wait(row_sem, 1)

    @pl.loop(0, NBD)
    def _(b):
        start = scaled_ref[LEV - 1, b]
        out_ref[LEV - 1, b] = jnp.where(keep, start, 0.0).astype(jnp.bfloat16)

        def substitute(count, below):
            level = LEV - 2 - count
            value = scaled_ref[level, b] + ratio_ref[level] * below
            out_ref[level, b] = jnp.where(keep, value, 0.0).astype(jnp.bfloat16)
            return value

        lax.fori_loop(0, LEV - 1, substitute, start)

        @pl.when(b == 0)
        def _():
            salt_copy.start()

        for step in ORDER:
            a2a_copy(b, step).start()
        own_copy(b).start()

    for load in tables:
        load.wait()
    salt_copy.wait()
    salt_ref[...] = (part_ref[...] + other_ref[...]) * valid

    @pl.loop(0, NBD)
    def _(b):
        arrived = recv_ref.at[:, :, b]
        pltpu.make_async_copy(arrived, arrived, a2a_recv.at[b]).wait()
        transform(recv_ref.at[:, :, b], twiddle_ref, table_ref, spectra_ref.at[:, b], z_ref, o_ref)

    sent = out_ref.at[pl.ds(0, 2 * (TILES - 1))]
    pltpu.make_async_copy(sent, sent, a2a_send).wait()


def deliver_kernel(from_spectra, from_salt, to_spectra, to_salt, sems):
    copies = [
        pltpu.make_async_copy(from_spectra, to_spectra, sems.at[0]),
        pltpu.make_async_copy(from_salt, to_salt, sems.at[1]),
    ]
    for copy in copies:
        copy.start()
    for copy in copies:
        copy.wait()


def deliver(spectra, salt):
    anywhere = pl.BlockSpec(memory_space=pl.ANY)
    vmem = pl.BlockSpec(memory_space=pltpu.VMEM)
    return pl.pallas_call(
        deliver_kernel,
        name="deliver",
        out_shape=tuple(jax.ShapeDtypeStruct(a.shape, a.dtype) for a in (spectra, salt)),
        in_specs=[anywhere] * 2,
        out_specs=(anywhere, anywhere),
        scratch_shapes=[pltpu.SemaphoreType.DMA((2,))],
        compiler_params=pltpu.CompilerParams(vmem_limit_bytes=2**20),
    )(spectra, salt)


def fused(*operands):
    vmem = pl.BlockSpec(memory_space=pltpu.VMEM)
    anywhere = pl.BlockSpec(memory_space=pl.ANY)
    dma = pltpu.SemaphoreType.DMA
    return pl.pallas_call(
        fused_kernel,
        name="fused",
        out_shape=(
            jax.ShapeDtypeStruct((2, NBD, ROWS, 2, K), jnp.float32),
            jax.ShapeDtypeStruct((ROWS, PTS), jnp.float32),
        ),
        in_specs=[pl.BlockSpec(memory_space=pltpu.HBM)] * 13,
        out_specs=(vmem, vmem),
        scratch_shapes=[
            pltpu.VMEM((4, 2, 128), jnp.bfloat16),
            pltpu.SMEM((1, 2), jnp.int32),
            pltpu.SMEM((1, 4, 8), jnp.int32),
            pltpu.SMEM((ROWS,), jnp.int32),
            pltpu.SMEM((NBD,), jnp.float32),
            pltpu.SMEM((NBD,), jnp.float32),
            pltpu.SMEM((NBD,), jnp.float32),
            pltpu.VMEM((2, ROWS, PTS), jnp.float32),
            pltpu.VMEM((ROWS, 4, 128, PTS), jnp.bfloat16),
            pltpu.VMEM((LEV, NBD, ROWS, PTS), jnp.bfloat16),
            pltpu.VMEM((LEV, ROWS, PTS), jnp.float32),
            pltpu.VMEM((TILES, 2, PTS), jnp.float32),
            pltpu.VMEM((4 * PTS, 256), jnp.bfloat16),
            pltpu.VMEM((12, 8, 128), jnp.float32),
            pltpu.VMEM((ROWS, 8, 512), jnp.float32),
            pltpu.VMEM((ROWS, 8, PTS), jnp.float32),
            pltpu.VMEM((LEV, ROWS, PTS), jnp.float32),
            pltpu.VMEM((LEV, NBD, ROWS, PTS), jnp.float32),
            pltpu.VMEM((LEV, NBD, ROWS, PTS), jnp.bfloat16),
            pltpu.VMEM((TILES, 2, NBD, ROWS, PTS), jnp.bfloat16),
            pltpu.VMEM((ROWS, PTS), jnp.float32),
            pltpu.VMEM((ROWS, PTS), jnp.float32),
            pltpu.VMEM((TILES, 16, 4 * PTS), jnp.bfloat16),
            pltpu.VMEM((TILES, 16, 256), jnp.float32),
            dma((13,)),
            dma,
            dma,
            dma,
            dma,
            dma,
            dma((NBD,)),
            pltpu.SemaphoreType.REGULAR,
        ],
        compiler_params=pltpu.CompilerParams(
            collective_id=0, has_side_effects=True, vmem_limit_bytes=16 * 2**20
        ),
    )(*[pltpu.with_memory_space_constraint(a, pltpu.HBM) for a in operands])


def twiddles():
    phase = np.arange(TILES)[:, None] * np.arange(PTS)[None, :] * (2.0 * np.pi / M)
    parts = np.stack([np.cos(phase), np.sin(phase)], axis=1) * (1.0 / math.sqrt(M))
    return parts.astype(np.float32)


def row_table():
    column = np.arange(256)
    combo = (column // 128) * 16 + column % 16
    ka = 8 * (combo // 2) + (column % 128) // 16
    phase = np.arange(PTS)[:, None] * ka[None, :] % PTS * (2.0 * np.pi / PTS)
    cos, sin = np.cos(phase), np.sin(phase)
    is_cos = (combo % 2 == 0)[None, :]
    upper = np.where(is_cos, cos, -sin)
    lower = np.where(is_cos, -sin, -cos)
    table = np.concatenate([upper, lower], axis=0) * (combo < 20)[None, :]
    return table.astype(np.float32)


def real_dft16(x):
    c1, c2, c3 = math.cos(math.pi / 8), math.cos(math.pi / 4), math.cos(3 * math.pi / 8)
    s = [x[i] + x[i + 8] for i in range(8)]
    d = [x[i] - x[i + 8] for i in range(8)]
    a = [s[i] + s[i + 4] for i in range(4)]
    b = [s[i] - s[i + 4] for i in range(4)]
    out = [None] * 9
    a02, a13 = a[0] + a[2], a[1] + a[3]
    out[0] = (a02 + a13, None)
    out[8] = (a02 - a13, None)
    out[4] = (a[0] - a[2], a[1] - a[3])
    bm, bp = (b[1] - b[3]) * c2, (b[1] + b[3]) * c2
    out[2] = (b[0] + bm, bp + b[2])
    out[6] = (b[0] - bm, bp - b[2])
    e1, e2, e3 = d[1] - d[7], (d[2] - d[6]) * c2, d[3] - d[5]
    f1, f2, f3 = d[1] + d[7], (d[2] + d[6]) * c2, d[3] + d[5]
    p, q = d[0] + e2, d[0] - e2
    u, v = e1 * c1 + e3 * c3, e1 * c3 - e3 * c1
    g, h = f1 * c3 + f3 * c1, f1 * c1 - f3 * c3
    m, n = f2 + d[4], f2 - d[4]
    out[1] = (p + u, g + m)
    out[7] = (p - u, g - m)
    out[3] = (q + v, h + n)
    out[5] = (q - v, h - n)
    return out


def transform(x_ref, twiddle_ref, table_ref, y_ref, z_ref, o_ref):
    for half in range(2):
        lanes = slice(half * 128, (half + 1) * 128)
        x = [
            x_ref[tile, :, :, lanes].astype(jnp.float32).reshape(16, 128)
            for tile in range(TILES)
        ]
        coefficients = real_dft16(x)
        for kb in range(TILES):
            re, im = coefficients[min(kb, TILES - kb)]
            cos = twiddle_ref[kb, 0:1, lanes]
            sin = twiddle_ref[kb, 1:2, lanes]
            if im is None:
                real, minus = re * cos, re * sin
            elif kb < 8:
                real, minus = re * cos - im * sin, re * sin + im * cos
            else:
                real, minus = re * cos + im * sin, re * sin - im * cos
            for part, value in enumerate((real, minus)):
                high = value.astype(jnp.bfloat16)
                low = (value - high.astype(jnp.float32)).astype(jnp.bfloat16)
                at = part * PTS + half * 128
                z_ref[kb, :, at : at + 128] = high
                z_ref[kb, :, 2 * PTS + at : 2 * PTS + at + 128] = low
    o_ref[...] = jnp.dot(
        z_ref[...].reshape(TILES * 16, 4 * PTS), table_ref[...], preferred_element_type=jnp.float32
    ).reshape(TILES, 16, 256)
    lane = lax.broadcasted_iota(jnp.int32, (8, 128), 1)
    for group in range(2):
        for q in range(2):
            combos = 16 if q == 0 else 4
            arrays = {
                kb: pltpu.roll(
                    o_ref[kb, group * 8 : (group + 1) * 8, q * 128 : (q + 1) * 128], kb, axis=1
                )
                for kb in range(TILES)
            }
            wanted = {(-t) % TILES for t in range(combos)}
            needs = [wanted]
            for bit in (0, 1, 2):
                wanted = wanted | {(j + (1 << bit)) % TILES for j in wanted}
                needs.append(wanted)
            for bit in (3, 2, 1, 0):
                taken = (lane & (1 << bit)) != 0
                arrays = {
                    j: jnp.where(taken, arrays[(j + (1 << bit)) % TILES], arrays[j])
                    for j in needs[bit]
                }
            for t in range(combos):
                value = arrays[(-t) % TILES]
                if t:
                    value = pltpu.roll(value, 128 - t, axis=1)
                c, part = divmod(q * 16 + t, 2)
                y_ref[group, :, part, c * 128 : (c + 1) * 128] = value


def on_device(
    ocean_state,
    sea_tiles,
    regrid_weights,
    regrid_src,
    row_points,
    wind,
    conc,
    kdiff,
    bin_emit,
    bin_settle,
    bin_mass,
):
    table = jnp.asarray(row_table()).astype(jnp.bfloat16)
    spectra, salt = fused(
        ocean_state.reshape(4, 2, 128),
        sea_tiles.reshape(1, 2),
        jnp.transpose(regrid_src, (1, 2, 0)),
        row_points,
        bin_emit,
        bin_settle,
        bin_mass,
        wind,
        regrid_weights,
        conc,
        kdiff,
        jnp.asarray(twiddles()),
        jnp.concatenate([table, table], axis=0),
    )
    return deliver(spectra, salt)


def solution(mesh):
    return jax.shard_map(
        on_device,
        mesh=mesh,
        in_specs=(
            P(None, "sec", "lat", "lon", None),
            P("sec", "lat", "lon"),
            P("lat", None, None, "lon"),
            P("lat", "lon", None),
            P("lat"),
            P(None, "lat", "lon"),
            P(None, "sec", "lat", "lon"),
            P(None, "lat", "lon"),
            P("sec"),
            P("sec"),
            P("sec"),
        ),
        out_specs=(P("lon", "sec", "lat", None, None), P("lat", "lon")),
        check_vma=False,
    )
```
